256 devices in a mesh: phi: 128 (over z, y, x_lo, core), row: 2 (over x_hi).
Axes of the slice: x: 4 (x_hi: 2, x_lo: 2; x = x_hi * 2 + x_lo), y: 4, z: 8, core: 2. Of those that a mesh axis runs over, the one named last changes fastest.
Arguments:
- density: float32 [2, 4096, 512], P(None, 'phi', 'row'), may hold values from 0.6 to 1.8
- momentum: float32 [2, 2, 4096, 512], P(None, None, 'phi', 'row'), may hold values from -1 to 1
- magnetic: float32 [2, 2, 4096, 512], P(None, None, 'phi', 'row'), may hold values from -1 to 1
- rotation: float32 [512], P('row'), may hold values from 1 to 4
- shifts: int32 [512], P('row'), may hold values from 8 to 56, as said below
Outputs:
- density_out: float32 [2, 4096, 512], P(None, 'phi', 'row')
- momentum_out: float32 [2, 2, 4096, 512], P(None, None, 'phi', 'row')
- magnetic_out: float32 [2, 2, 4096, 512], P(None, None, 'phi', 'row')
The draws below stay inside these ranges and needn't reach their ends.
Inputs may be any that keep to these rules, and one draw needn't show every extreme that they name: shifts[r] = 8 + floor((47) d^2 / 511^2) + j_r with d = 511 - r and j_r either 0 or 1, except that row 0 shifts by exactly 56 and the last row by exactly 8.
All inputs are finite; a program needn't handle non-finite values.
Results may differ from the reference program's by a relative error of at most 0.0003.
Values sent between devices are 32-bit elements; how exact they have to be, the bound alone decides.
A program may use at most 64 MiB of HBM per device.

```python
import math
import jax
import jax.numpy as jnp
from jax import lax

CPHI = 32
LEVELS = 2
STEPS = 2
SMIN = 8
SMAX = 56
NPHI = 4096
NR = 512


def draw_shifts(key, part):
    radius_rows = jnp.arange(NR, dtype=jnp.int32)
    distance = NR - 1 - radius_rows
    spread = SMAX - SMIN - 1
    smooth_part = SMIN + spread * distance * distance // ((NR - 1) * (NR - 1))
    jitter = jax.random.randint(key, (NR,), 0, 2, dtype=jnp.int32)
    values = smooth_part + jitter
    values = values.at[0].set(SMAX).at[NR - 1].set(SMIN)
    return values.astype(jnp.int32)


def band_layout():
    radius_rows = jnp.arange(NR, dtype=jnp.int32)
    phi_cells = jnp.arange(NPHI, dtype=jnp.int32)
    middle = NR // 2
    radial_band = jnp.logical_and(radius_rows >= middle - 12, radius_rows < middle + 12)
    offset = phi_cells % CPHI
    phi_band = jnp.logical_or(offset < 6, offset >= CPHI - 6)
    radial_flip = jnp.where(radial_band, 1.0 - 2.0 * (radius_rows % 2).astype(jnp.float32), 1.0)
    phi_flip = jnp.where(phi_band, 1.0 - 2.0 * (phi_cells % 2).astype(jnp.float32), 1.0)
    pattern = phi_flip[:, None] * radial_flip[None, :]
    radial_mask = jnp.broadcast_to(radial_band[None, :], (NPHI, NR))
    phi_mask = jnp.broadcast_to(phi_band[:, None], (NPHI, NR))
    return (radial_mask, phi_mask, pattern)


def random_sign(key, shape):
    return jax.random.randint(key, shape, 0, 2, dtype=jnp.int32).astype(jnp.float32) * 2.0 - 1.0


def band_signs(key, leading):
    radial_mask, phi_mask, pattern = band_layout()
    keys = jax.random.split(key, 3)
    along_phi = random_sign(keys[0], leading + (NPHI, 1))
    along_rad = random_sign(keys[1], leading + (1, NR))
    shared = random_sign(keys[2], leading + (1, 1))
    both = jnp.logical_and(radial_mask, phi_mask)
    chosen = jnp.where(both, shared, jnp.where(radial_mask, along_phi, along_rad))
    return (chosen * pattern, jnp.logical_or(radial_mask, phi_mask))


def draw_density(key, part):
    base = jax.random.fold_in(key, 11)
    keys = jax.random.split(base, 4)
    shape = (LEVELS, NPHI, NR)
    signs, band_mask = band_signs(keys[0], (LEVELS,))
    high = jax.random.uniform(keys[1], shape, jnp.float32, 1.5, 1.8)
    low = jax.random.uniform(keys[2], shape, jnp.float32, 0.6, 0.8)
    banded = jnp.where(signs > 0.0, high, low)
    drawn = jax.random.uniform(keys[3], shape, jnp.float32, 0.6, 1.8)
    return jnp.where(band_mask[None], banded, drawn).astype(jnp.float32)


def draw_momentum(key, part):
    base = jax.random.fold_in(key, 23)
    keys = jax.random.split(base, 3)
    shape = (2, LEVELS, NPHI, NR)
    signs, band_mask = band_signs(keys[0], (2, LEVELS))
    banded = signs * jax.random.uniform(keys[1], shape, jnp.float32, 0.6, 1.0)
    drawn = jnp.clip(0.3 * jax.random.normal(keys[2], shape, jnp.float32), -1.0, 1.0)
    return jnp.where(band_mask[None, None], banded, drawn).astype(jnp.float32)


def draw_magnetic(key, part):
    base = jax.random.fold_in(key, 37)
    keys = jax.random.split(base, 3)
    shape = (2, LEVELS, NPHI, NR)
    signs, band_mask = band_signs(keys[0], (2, LEVELS))
    banded = signs * jax.random.uniform(keys[1], shape, jnp.float32, 0.6, 1.0)
    drawn = jnp.clip(0.3 * jax.random.normal(keys[2], shape, jnp.float32), -1.0, 1.0)
    return jnp.where(band_mask[None, None], banded, drawn).astype(jnp.float32)


def level_of(rng, extent, shards, least, high):
    factor_of, own = 1.0, jax.random.fold_in(rng, 6)
    for position, parts in shards:
        draws = jnp.exp(jax.random.uniform(jax.random.fold_in(own, position), (parts,), jnp.float32, least / len(shards), high / len(shards)))
        factor_of = factor_of * jnp.repeat(draws, extent[position] // parts).reshape([-1 if axis == position else 1 for axis in range(len(extent))])
    return factor_of


def setup_inputs(seed: int = 0) -> dict:
    splits = jax.random.split(jax.random.key(seed), 6)
    return {
        "density": draw_density(jax.random.fold_in(splits[5], 71), 0),
        "momentum": draw_momentum(jax.random.fold_in(splits[5], 71), 0),
        "magnetic": draw_magnetic(jax.random.fold_in(splits[5], 71), 0),
        "rotation": jnp.clip(jnp.exp(math.log(4.0) - 1.3862944 * jax.random.uniform(splits[3], (NR,), jnp.float32) ** level_of(splits[3], (NR,), ((0, 2),), -0.2, 0.2)), 1.0, 4.0),
        "shifts": draw_shifts(jax.random.fold_in(splits[5], 71), 0),
    }


time_step = 0.08
sound_sq = 1.0
block_rows = 128

def window(values, begin_at, end_at, along_axis):
    return lax.slice_in_dim(values, begin_at, values.shape[along_axis] + end_at, 1, along_axis)

def minmod(lower_jump, upper_jump):
    return 0.5 * (jnp.sign(lower_jump) + jnp.sign(upper_jump)) * jnp.minimum(jnp.abs(lower_jump), jnp.abs(upper_jump))

def physical(fields, normal):
    density, mom_phi, mom_rad, mag_phi, mag_rad = (fields[0], fields[1], fields[2], fields[3], fields[4])
    vel_phi = mom_phi / density
    vel_rad = mom_rad / density
    magnetic_sq = mag_phi * mag_phi + mag_rad * mag_rad
    pressure = sound_sq * density + 0.5 * magnetic_sq
    nothing = jnp.zeros_like(density)
    if normal == 0:
        fluxes = jnp.stack([mom_phi, mom_phi * vel_phi + pressure - mag_phi * mag_phi, mom_rad * vel_phi - mag_phi * mag_rad, nothing, mag_rad * vel_phi - mag_phi * vel_rad])
        normal_vel = vel_phi
    else:
        fluxes = jnp.stack([mom_rad, mom_phi * vel_rad - mag_phi * mag_rad, mom_rad * vel_rad + pressure - mag_rad * mag_rad, mag_phi * vel_rad - mag_rad * vel_phi, nothing])
        normal_vel = vel_rad
    speeds = jnp.abs(normal_vel) + jnp.sqrt(sound_sq + magnetic_sq / density)
    return (fluxes, speeds)

def interfaces(fields, along_axis, normal):
    differences = window(fields, 1, 0, along_axis) - window(fields, 0, -1, along_axis)
    slopes = minmod(window(differences, 0, -1, along_axis), window(differences, 1, 0, along_axis))
    centres = window(fields, 1, -1, along_axis)
    left_state = window(centres + 0.5 * slopes, 0, -1, along_axis)
    right_state = window(centres - 0.5 * slopes, 1, 0, along_axis)
    left_flux, left_speed = physical(left_state, normal)
    right_flux, right_speed = physical(right_state, normal)
    wave_bound = jnp.maximum(left_speed, right_speed)
    return 0.5 * (left_flux + right_flux) - 0.5 * wave_bound * (right_state - left_state)

def tendency(along_phi, along_rad, rotation):
    phi_flux = interfaces(along_phi, 2, 0)
    rad_flux = interfaces(along_rad, 3, 1)
    centre = window(along_phi, 2, -2, 2)
    change = -(window(phi_flux, 1, 0, 2) - window(phi_flux, 0, -1, 2)) - (window(rad_flux, 1, 0, 3) - window(rad_flux, 0, -1, 3))
    spin_rate = rotation[None, None, :]
    nothing = jnp.zeros_like(centre[0])
    source = jnp.stack([nothing, -0.5 * spin_rate * centre[2], 2.0 * spin_rate * centre[1], -1.5 * spin_rate * centre[4], nothing])
    return change + source

def blocked(fields, rotation):
    along_phi_all = jnp.concatenate([fields[:, :, -2:], fields, fields[:, :, :2]], axis=2)
    along_rad_all = jnp.concatenate([fields[..., :1], fields[..., :1], fields, fields[..., -1:], fields[..., -1:]], axis=3)
    block_count = NR // block_rows

    def one_block(number):
        first_row = number * block_rows
        phi_part = lax.dynamic_slice_in_dim(along_phi_all, first_row, block_rows, 3)
        rad_part = lax.dynamic_slice_in_dim(along_rad_all, first_row, block_rows + 4, 3)
        spin_part = lax.dynamic_slice_in_dim(rotation, first_row, block_rows, 0)
        return tendency(phi_part, rad_part, spin_part)
    result = lax.map(one_block, jnp.arange(block_count, dtype=jnp.int32))
    return jnp.moveaxis(result, 0, 3).reshape(fields.shape)

def fargo_shift(fields, shifts):
    cell_ids = jnp.arange(NPHI, dtype=jnp.int32)
    source_cell = (cell_ids[:, None] - shifts[None, :]) % NPHI
    return jnp.take_along_axis(fields, jnp.broadcast_to(source_cell, fields.shape), axis=2)

def reference(density, momentum, magnetic, rotation, shifts):
    fields = jnp.concatenate([density[None], momentum, magnetic], axis=0)
    for step_number in range(STEPS):
        first_section = fields + time_step * blocked(fields, rotation)
        second_section = 0.75 * fields + 0.25 * (first_section + time_step * blocked(first_section, rotation))
        third_section = fields / 3.0 + 2.0 / 3.0 * (second_section + time_step * blocked(second_section, rotation))
        fields = fargo_shift(third_section, shifts)
    return (fields[0], fields[1:3], fields[3:5])
```

```python
import jax
import jax.numpy as jnp
import numpy as np
from jax import lax
from jax.experimental import pallas as pl
from jax.experimental.pallas import tpu as pltpu
from jax.sharding import PartitionSpec as P

SMIN, SMAX = 8, 56
NR = 512
DT = 0.08
LV, NC, CELLS, HALO, LANES = 2, 5, 32, 8, 128
ROWS = CELLS + 2 * HALO
TALL = 64
OWN = 128
ZTALL = 232
HOPS = 4
MESH = pl.DeviceIdType.MESH
F32 = jnp.float32


def smooth(rows):
    d = NR - 1 - np.clip(rows, 0, NR - 1)
    return SMIN + ((SMAX - SMIN - 1) * d * d) // ((NR - 1) * (NR - 1))


def tables():
    table = np.zeros((2, 16, LANES), np.float32)
    lanes = np.arange(LANES)
    for row in range(2):
        first = row * 256
        strip = np.where(lanes < 64, first + 256 + lanes, first - LANES + lanes)
        for k, r in enumerate((first + lanes, first + LANES + lanes, strip)):
            table[row, k] = smooth(r - 1) - smooth(r)
            table[row, 3 + k] = smooth(r) - smooth(r + 1)
            table[row, 6 + k] = smooth(r)
    return table


def pieces():
    plan = {}
    for row in range(2):
        for ch in range(2):
            b = smooth(row * 256 + ch * LANES + np.arange(LANES))
            low, high = int(2 * b.min()), int(2 * b.max() + 1)
            moves = []
            for k in range(1, HOPS + 1):
                begin = max(0, CELLS * k - high)
                end = min(CELLS, CELLS - low + CELLS * k)
                if begin < end:
                    moves.append((k, begin // 8 * 8, -(-end // 8) * 8))
            base = (112 - high) // 8 * 8
            plan[row, ch] = (base, tuple(moves))
    return plan


def minmod(a, b):
    return jnp.maximum(jnp.minimum(a, b), 0.0) + jnp.minimum(jnp.maximum(a, b), 0.0)


def physical(state, normal):
    rho, mp, mr, bp, br = state
    inv = 1.0 / rho
    mn, mt, bn, bt = (mp, mr, bp, br) if normal == 0 else (mr, mp, br, bp)
    vn, vt = mn * inv, mt * inv
    bn2, bt2 = bn * bn, bt * bt
    fn = mn * vn + (rho + 0.5 * (bt2 - bn2))
    ft = mt * vn - bn * bt
    fb = bt * vn - bn * vt
    fast = 1.0 + (bn2 + bt2) * inv
    speed = jnp.abs(vn) + fast * lax.rsqrt(fast)
    flux = (mn, fn, ft, None, fb) if normal == 0 else (mn, ft, fn, fb, None)
    return flux, speed


def twice_face(left, right, normal):
    fl, al = physical(left, normal)
    fr, ar = physical(right, normal)
    bound = jnp.maximum(al, ar)
    out = []
    for c in range(NC):
        jump = bound * (right[c] - left[c])
        out.append(-jump if fl[c] is None else (fl[c] + fr[c]) - jump)
    return out


def kernel(den, mom, mag, aux, tab, o_den, o_mom, o_mag,
           u0, ua, ub, res, land, edge, edge2, paux, hp, rr, gp, gr, masks, spin,
           send1, recv1, send2, recv2, send3, recv3, sendx, recvx):
    phi, row = lax.axis_index("phi"), lax.axis_index("row")
    n = lax.axis_size("phi")
    other = 1 - row

    def at(step, r):
        return {"phi": lax.rem(phi + step + n, n), "row": r}

    barrier = pltpu.get_barrier_semaphore()
    greet = [at(k, row) for k in (1, -1, 2, -2, 3, -3, 4, -4)]
    greet += [at(0, other), at(1, other), at(-1, other)]
    for dev in greet:
        pl.semaphore_signal(barrier, inc=1, device_id=dev, device_id_type=MESH)

    lane = lax.broadcasted_iota(jnp.int32, (8, LANES), 1)
    first_lane, last_lane = lane == 0, lane == LANES - 1
    ghost = jnp.logical_or(
        jnp.logical_and(row == 0, lane >= LANES - 2), jnp.logical_and(row == 1, lane < 2)
    )

    def source(lv, c):
        if c == 0:
            return den.at[lv]
        return mom.at[c - 1, lv] if c < 3 else mag.at[c - 3, lv]

    def pack_edges(ref, dst, lv, offset):
        for c in range(NC):
            for t in range(CELLS // 8):
                rows = pl.ds(offset + 8 * t, 8)
                dst[lv, c, pl.ds(8 * t, 8), :] = jnp.where(
                    lane < 64, ref[lv, c, 0, rows, :], ref[lv, c, 1, rows, :]
                )

    for lv in range(LV):
        for c in range(NC):
            src = source(lv, c)
            for ch in range(2):
                for t in range(CELLS // 8):
                    u0[lv, c, ch, pl.ds(HALO + 8 * t, 8), :] = src[
                        pl.ds(8 * t, 8), pl.ds(LANES * ch, LANES)
                    ]
        pack_edges(u0, edge, lv, HALO)
    for k in range(9):
        masks[k] = jnp.broadcast_to(tab[row, pl.ds(k, 1), :], (8, LANES))

    pl.semaphore_wait(barrier, len(greet))

    def remote(src, dst, send, recv, dev):
        return pltpu.make_async_remote_copy(
            src_ref=src, dst_ref=dst, send_sem=send, recv_sem=recv, device_id=dev, device_id_type=MESH
        )

    def halo_copies(buf, packed, lv, send, recv):
        top, bottom = pl.ds(HALO + CELLS - 8, 8), pl.ds(HALO, 8)
        above, below = pl.ds(HALO + CELLS, 8), pl.ds(0, 8)
        main = pl.ds(0, 2)
        return [
            remote(buf.at[lv, :, main, top, :], buf.at[lv, :, main, below, :], send.at[lv, 0], recv.at[lv, 0], at(1, row)),
            remote(buf.at[lv, :, main, bottom, :], buf.at[lv, :, main, above, :], send.at[lv, 1], recv.at[lv, 1], at(-1, row)),
            remote(packed.at[lv], buf.at[lv, :, 2, pl.ds(HALO, CELLS), :], send.at[lv, 2], recv.at[lv, 2], at(0, other)),
            remote(packed.at[lv, :, pl.ds(CELLS - 8, 8), :], buf.at[lv, :, 2, below, :], send.at[lv, 3], recv.at[lv, 3], at(1, other)),
            remote(packed.at[lv, :, pl.ds(0, 8), :], buf.at[lv, :, 2, above, :], send.at[lv, 4], recv.at[lv, 4], at(-1, other)),
        ]

    auxcopy = remote(aux, paux, sendx, recvx, at(0, other))
    auxcopy.start()
    first = [halo_copies(u0, edge, lv, send1, recv1) for lv in range(LV)]
    for copies in first:
        for cp in copies:
            cp.start()

    def edge_fill(c0, c1, strip):
        edge_value = jnp.where(
            row == 0,
            jnp.broadcast_to(c0[:, :1], (8, LANES)),
            jnp.broadcast_to(c1[:, LANES - 1 :], (8, LANES)),
        )
        return jnp.where(ghost, edge_value, strip)

    def forward(values):
        rolled = [pltpu.roll(v, LANES - 1, 1) for v in values]
        return [jnp.where(last_lane, rolled[(k + 1) % 3], rolled[k]) for k in range(3)]

    def backward(values):
        rolled = [pltpu.roll(v, 1, 1) for v in values]
        return [jnp.where(first_lane, rolled[(k + 2) % 3], rolled[k]) for k in range(3)]

    def loop(count, body):
        lax.fori_loop(0, count, lambda i, _: (body(i), 0)[1], 0)

    def stage(lv, cur, old, dst, margin, a, c0, sheared, last):
        begin, end = HALO - margin, HALO + CELLS + margin

        def nxt(ref, c, o, lead=()):
            out = []
            for k in range(3):
                v = ref[(*lead, c, k, pl.ds(o, 8), slice(None))]
                if sheared:
                    v = jnp.where(masks[k] > 0.5, ref[(*lead, c, k, pl.ds(o + 1, 8), slice(None))], v)
                out.append(v)
            return forward(out)

        def prv(ref, c, o, lead=()):
            out = []
            for k in range(3):
                v = ref[(*lead, c, k, pl.ds(o, 8), slice(None))]
                if sheared:
                    v = jnp.where(masks[3 + k] > 0.5, ref[(*lead, c, k, pl.ds(o - 1, 8), slice(None))], v)
                out.append(v)
            return backward(out)

        def slopes(i):
            o = begin - 1 + 8 * i
            for c in range(NC):
                ahead, behind = nxt(cur, c, o, (lv,)), prv(cur, c, o, (lv,))
                for k in range(3):
                    u = cur[lv, c, k, pl.ds(o, 8), :]
                    up = cur[lv, c, k, pl.ds(o + 1, 8), :]
                    um = cur[lv, c, k, pl.ds(o - 1, 8), :]
                    hp[c, k, pl.ds(o, 8), :] = 0.5 * minmod(u - um, up - u)
                    rr[c, k, pl.ds(o, 8), :] = u - 0.5 * minmod(u - behind[k], ahead[k] - u)

        def fluxes(i):
            o = begin - 1 + 8 * i
            right_of = [nxt(rr, c, o) for c in range(NC)]
            for k in range(3):
                here = [cur[lv, c, k, pl.ds(o, 8), :] for c in range(NC)]
                left = [here[c] + hp[c, k, pl.ds(o, 8), :] for c in range(NC)]
                right = [cur[lv, c, k, pl.ds(o + 1, 8), :] - hp[c, k, pl.ds(o + 1, 8), :] for c in range(NC)]
                for c, g in enumerate(twice_face(left, right, 0)):
                    gp[c, k, pl.ds(o, 8), :] = g
                left = [here[c] + (here[c] - rr[c, k, pl.ds(o, 8), :]) for c in range(NC)]
                right = [right_of[c][k] for c in range(NC)]
                for c, g in enumerate(twice_face(left, right, 1)):
                    gr[c, k, pl.ds(o, 8), :] = g

        chunks = 2 if last else 3

        def update(i):
            o = begin + 8 * i
            here = [[cur[lv, c, k, pl.ds(o, 8), :] for k in range(chunks)] for c in range(NC)]
            turn = [spin[k] for k in range(chunks)]
            for c in range(NC):
                below = prv(gr, c, o)
                news = []
                for k in range(chunks):
                    change = (gp[c, k, pl.ds(o, 8), :] - gp[c, k, pl.ds(o - 1, 8), :]) + (
                        gr[c, k, pl.ds(o, 8), :] - below[k]
                    )
                    new = c0 * here[c][k] - (0.5 * DT * c0) * change
                    if a:
                        new = new + a * old[lv, c, k, pl.ds(o, 8), :]
                    if c == 1:
                        new = new - (0.5 * DT * c0) * turn[k] * here[2][k]
                    elif c == 2:
                        new = new + (2.0 * DT * c0) * turn[k] * here[1][k]
                    elif c == 3:
                        new = new - (1.5 * DT * c0) * turn[k] * here[4][k]
                    news.append(new)
                if not last:
                    news[2] = edge_fill(*news)
                for k in range(chunks):
                    dst(c, k, o, news[k])

        loop(-(-(end - begin + 2) // 8), slopes)
        loop(-(-(end - begin + 2) // 8), fluxes)
        loop(-(-(end - begin) // 8), update)

    def step(lv, sheared, final):
        def into(ref):
            def put(c, k, o, value):
                ref[lv, c, k, pl.ds(o, 8), :] = value
            return put

        def put_final(c, k, o, value):
            land[lv, c, k, pl.ds(o + (OWN - HALO), 8), :] = value

        stage(lv, u0, u0, into(ua), 4, 0.0, 1.0, sheared, False)
        stage(lv, ua, u0, into(ub), 2, 0.75, 0.25, sheared, False)
        stage(lv, ub, u0, put_final if final else into(res), 0, 1.0 / 3.0, 2.0 / 3.0, sheared, True)

    def fill_ghosts(ref, lv):
        def body(t):
            rows = pl.ds(8 * t, 8)
            for c in range(NC):
                ref[lv, c, 2, rows, :] = edge_fill(
                    ref[lv, c, 0, rows, :], ref[lv, c, 1, rows, :], ref[lv, c, 2, rows, :]
                )
        loop(ROWS // 8, body)

    auxcopy.wait()
    for k in range(2):
        spin[k] = jnp.broadcast_to(aux[pl.ds(k, 1), :], (8, LANES))
    spin[2] = jnp.where(
        lane < 64,
        jnp.broadcast_to(paux[pl.ds(0, 1), :], (8, LANES)),
        jnp.broadcast_to(paux[pl.ds(1, 1), :], (8, LANES)),
    )
    shift_of = [jnp.broadcast_to(aux[pl.ds(2 + k, 1), :], (8, LANES)) for k in range(2)]
    shift_of.append(
        jnp.where(
            lane < 64,
            jnp.broadcast_to(paux[pl.ds(2, 1), :], (8, LANES)),
            jnp.broadcast_to(paux[pl.ds(3, 1), :], (8, LANES)),
        )
    )
    for k in range(3):
        masks[9 + k] = shift_of[k] - masks[6 + k]
    second = [halo_copies(res, edge2, lv, send2, recv2) for lv in range(LV)]
    for lv in range(LV):
        for cp in first[lv]:
            cp.wait()
        fill_ghosts(u0, lv)
        step(lv, False, False)
        pack_edges(res, edge2, lv, HALO)
        for cp in second[lv]:
            cp.start()

    plan = pieces()

    def bulk(lv, row_id):
        out = []
        for ch in range(2):
            for k, r0, r1 in plan[row_id, ch][1]:
                rows = pl.ds(OWN + r0, r1 - r0)
                there = pl.ds(OWN - CELLS * k + r0, r1 - r0)
                out.append(remote(
                    land.at[lv, :, ch, rows, :], land.at[lv, :, ch, there, :],
                    send3.at[lv, ch, k - 1], recv3.at[lv, ch, k - 1], at(k, row),
                ))
        return out

    for lv in range(LV):
        for cp in second[lv]:
            cp.wait()

        def jitter(t):
            o = 1 + 8 * t
            for c in range(NC):
                news = [
                    jnp.where(masks[9 + k] > 0.5, res[lv, c, k, pl.ds(o - 1, 8), :], res[lv, c, k, pl.ds(o, 8), :])
                    for k in range(3)
                ]
                news[2] = edge_fill(*news)
                for k in range(3):
                    u0[lv, c, k, pl.ds(o, 8), :] = news[k]

        loop(ROWS // 8, jitter)
        step(lv, True, True)
        for row_id in range(2):
            @pl.when(row == row_id)
            def _():
                for cp in bulk(lv, row_id):
                    cp.start()

    def target(lv, c):
        if c == 0:
            return o_den.at[lv]
        return o_mom.at[c - 1, lv] if c < 3 else o_mag.at[c - 3, lv]

    for lv in range(LV):
        for row_id in range(2):
            @pl.when(row == row_id)
            def _():
                for cp in bulk(lv, row_id):
                    cp.wait()
        for ch in range(2):
            base = jnp.where(row == 0, plan[0, ch][0], plan[1, ch][0])
            start = OWN - 112 + base
            togo = (112 - base).astype(F32) - masks[6 + ch] - shift_of[ch]
            togo = togo.astype(jnp.int32)
            bits = [(lax.shift_right_logical(togo, b) & 1) == 1 for b in range(6)]
            for c in range(NC):
                tiles = [land[lv, c, ch, pl.ds(start + 8 * t, 8), :] for t in range(12)]
                for b in (5, 4, 3):
                    jump = 2 ** (b - 3)
                    tiles = [jnp.where(bits[b], tiles[t + jump], tiles[t]) for t in range(len(tiles) - jump)]
                for b in (2, 1, 0):
                    block = jnp.concatenate(tiles, axis=0)
                    moved = pltpu.roll(block, block.shape[0] - 2**b, 0)
                    tiles = [
                        jnp.where(bits[b], moved[8 * t : 8 * t + 8], tiles[t]) for t in range(len(tiles))
                    ]
                out = target(lv, c)
                for t in range(CELLS // 8):
                    out[pl.ds(8 * t, 8), pl.ds(LANES * ch, LANES)] = tiles[t]


def body(density, momentum, magnetic, rotation, shifts):
    aux = jnp.concatenate(
        [rotation.reshape(2, LANES), shifts.astype(F32).reshape(2, LANES), jnp.zeros((4, LANES), F32)]
    )
    block = pltpu.VMEM((LV, NC, 3, TALL, LANES), F32)
    flat = pltpu.VMEM((NC, 3, TALL, LANES), F32)
    packed = pltpu.VMEM((LV, NC, CELLS, LANES), F32)
    dma = pltpu.SemaphoreType.DMA
    vmem = pl.BlockSpec(memory_space=pltpu.VMEM)
    return pl.pallas_call(
        kernel,
        out_shape=tuple(jax.ShapeDtypeStruct(v.shape, F32) for v in (density, momentum, magnetic)),
        in_specs=[vmem] * 5,
        out_specs=(vmem,) * 3,
        scratch_shapes=[
            block, block, block, block,
            pltpu.VMEM((LV, NC, 2, ZTALL, LANES), F32),
            packed, packed,
            pltpu.VMEM((8, LANES), F32),
            flat, flat, flat, flat,
            pltpu.VMEM((12, 8, LANES), F32),
            pltpu.VMEM((3, 8, LANES), F32),
            dma((LV, 5)), dma((LV, 5)), dma((LV, 5)), dma((LV, 5)),
            dma((LV, 2, HOPS)), dma((LV, 2, HOPS)),
            dma, dma,
        ],
        compiler_params=pltpu.CompilerParams(collective_id=0, has_side_effects=True),
        name="mhd_steps",
    )(density, momentum, magnetic, aux, jnp.asarray(tables()))


def solution(mesh):
    placed = (
        P(None, "phi", "row"),
        P(None, None, "phi", "row"),
        P(None, None, "phi", "row"),
        P("row"),
        P("row"),
    )
    return jax.shard_map(
        body,
        mesh=mesh,
        in_specs=placed,
        out_specs=(P(None, "phi", "row"), P(None, None, "phi", "row"), P(None, None, "phi", "row")),
        check_vma=False,
    )
```

```python
import jax
import jax.numpy as jnp
import numpy as np
from jax import lax
from jax.experimental import pallas as pl
from jax.experimental.pallas import tpu as pltpu
from jax.sharding import PartitionSpec as P

SMIN, SMAX = 8, 56
NR = 512
DT = 0.08
LV, NC, CELLS, HALO, LANES = 2, 5, 32, 8, 128
ROWS = CELLS + 2 * HALO
TALL = 64
OWN = 64
LAND = 128
HOPS = 2
MESH = pl.DeviceIdType.MESH
F32 = jnp.float32


def smooth(rows):
    d = NR - 1 - np.clip(rows, 0, NR - 1)
    return SMIN + ((SMAX - SMIN - 1) * d * d) // ((NR - 1) * (NR - 1))


def pieces(ghosts):
    plan = {}
    for row in range(2):
        for ch in range(2):
            b = smooth(row * 256 + ch * LANES + np.arange(LANES))
            low, high = int(b.min()), int(b.max() + 1)
            moves = []
            for k in range(1, HOPS + 1):
                begin = max(0, CELLS * k - high - ghosts)
                end = min(CELLS, CELLS + ghosts - low + CELLS * k)
                if begin < end:
                    moves.append((k, begin // 8 * 8, -(-end // 8) * 8))
            plan[row, ch] = ((SMAX - high) // 8 * 8, tuple(moves))
    return plan


def minmod(a, b):
    return jnp.maximum(jnp.minimum(a, b), 0.0) + jnp.minimum(jnp.maximum(a, b), 0.0)


def physical(state, normal):
    rho, mp, mr, bp, br = state
    inv = 1.0 / rho
    mn, mt, bn, bt = (mp, mr, bp, br) if normal == 0 else (mr, mp, br, bp)
    vn, vt = mn * inv, mt * inv
    bn2, bt2 = bn * bn, bt * bt
    fn = mn * vn + (rho + 0.5 * (bt2 - bn2))
    ft = mt * vn - bn * bt
    fb = bt * vn - bn * vt
    fast = 1.0 + (bn2 + bt2) * inv
    speed = jnp.abs(vn) + fast * lax.rsqrt(fast)
    flux = (mn, fn, ft, None, fb) if normal == 0 else (mn, ft, fn, fb, None)
    return flux, speed


def twice_face(left, right, normal):
    fl, al = physical(left, normal)
    fr, ar = physical(right, normal)
    bound = jnp.maximum(al, ar)
    out = []
    for c in range(NC):
        jump = bound * (right[c] - left[c])
        out.append(-jump if fl[c] is None else (fl[c] + fr[c]) - jump)
    return out


def kernel(den, mom, mag, rot, sft, out,
           u0, ua, ub, land1, land2, pack1, pack2, got1, got2, prot, psft, hp, rr, gp, gr, spin,
           send1, recv1, send2, recv2, send3, recv3, send4, recv4, sendx, recvx):
    phi, row = lax.axis_index("phi"), lax.axis_index("row")
    n = lax.axis_size("phi")
    other = 1 - row

    def at(step, r):
        return {"phi": lax.rem(phi + step + n, n), "row": r}

    barrier = pltpu.get_barrier_semaphore()
    greet = [at(k, row) for k in (1, -1, 2, -2)] + [at(k, other) for k in (0, 1, -1)]
    for dev in greet:
        pl.semaphore_signal(barrier, inc=1, device_id=dev, device_id_type=MESH)

    lane = lax.broadcasted_iota(jnp.int32, (8, LANES), 1)
    first_lane, last_lane = lane == 0, lane == LANES - 1
    ghost = jnp.logical_or(
        jnp.logical_and(row == 0, lane >= LANES - 2), jnp.logical_and(row == 1, lane < 2)
    )
    slot = [jnp.logical_and(lane >= 8 * c, lane < 8 * c + 8) for c in range(NC)]

    def source(lv, c):
        if c == 0:
            return den.at[lv]
        return mom.at[c - 1, lv] if c < 3 else mag.at[c - 3, lv]

    def loop(count, body):
        lax.fori_loop(0, count, lambda i, _: (body(i), 0)[1], 0)

    def pack_edges(ref, dst, lv, offset):
        for t in range(CELLS // 8):
            packed = jnp.zeros((8, LANES), F32)
            for c in range(NC):
                rows = pl.ds(offset + 8 * t, 8)
                side = jnp.where(row == 0, ref[lv, c, 1, rows, :], ref[lv, c, 0, rows, :])
                packed = jnp.where(slot[c], pltpu.roll(side, 8 * c + 8 * (1 - row), 1), packed)
            dst[lv, pl.ds(8 * t, 8), :] = packed

    def unpack(packed, c):
        return pltpu.roll(packed, LANES - 8 * c - 8 * row, 1)

    for lv in range(LV):
        for c in range(NC):
            src = source(lv, c)
            for ch in range(2):
                for t in range(CELLS // 8):
                    u0[lv, c, ch, pl.ds(HALO + 8 * t, 8), :] = src[
                        pl.ds(8 * t, 8), pl.ds(LANES * ch, LANES)
                    ]
        pack_edges(u0, pack1, lv, HALO)

    def remote(src, dst, send, recv, dev):
        return pltpu.make_async_remote_copy(
            src_ref=src, dst_ref=dst, send_sem=send, recv_sem=recv, device_id=dev, device_id_type=MESH
        )

    def first(lv):
        top, bottom = pl.ds(HALO + CELLS - 8, 8), pl.ds(HALO, 8)
        above, below = pl.ds(HALO + CELLS, 8), pl.ds(0, 8)
        main = pl.ds(0, 2)
        parts = (
            (u0.at[lv, :, main, top, :], u0.at[lv, :, main, below, :], at(1, row)),
            (u0.at[lv, :, main, bottom, :], u0.at[lv, :, main, above, :], at(-1, row)),
            (pack1.at[lv], got1.at[lv, pl.ds(HALO, CELLS), :], at(0, other)),
            (pack1.at[lv, pl.ds(CELLS - 8, 8), :], got1.at[lv, below, :], at(1, other)),
            (pack1.at[lv, pl.ds(0, 8), :], got1.at[lv, above, :], at(-1, other)),
        )
        return [remote(a, b, send1.at[lv, i], recv1.at[lv, i], dev) for i, (a, b, dev) in enumerate(parts)]

    def second(lv):
        parts = (
            (pack2.at[lv], got2.at[lv, pl.ds(CELLS, CELLS), :], at(0, other)),
            (pack2.at[lv], got2.at[lv, pl.ds(0, CELLS), :], at(1, other)),
        )
        return [remote(a, b, send2.at[lv, i], recv2.at[lv, i], dev) for i, (a, b, dev) in enumerate(parts)]

    def moved(land, plan, lv, row_id, send, recv):
        copies = []
        for ch in range(2):
            for k, r0, r1 in plan[row_id, ch][1]:
                here, there = pl.ds(OWN + r0, r1 - r0), pl.ds(OWN - CELLS * k + r0, r1 - r0)
                copies.append(remote(
                    land.at[lv, :, ch, here, :], land.at[lv, :, ch, there, :],
                    send.at[lv, ch, k - 1], recv.at[lv, ch, k - 1], at(k, row),
                ))
        return copies

    plan_mid, plan_end = pieces(6), pieces(0)

    def on_moved(land, plan, lv, send, recv, what):
        for row_id in range(2):
            @pl.when(row == row_id)
            def _():
                for cp in moved(land, plan, lv, row_id, send, recv):
                    getattr(cp, what)()

    pl.semaphore_wait(barrier, len(greet))
    tables = [
        remote(rot, prot, sendx.at[0], recvx.at[0], at(0, other)),
        remote(sft, psft, sendx.at[1], recvx.at[1], at(0, other)),
    ]
    for cp in first(0) + tables + first(1):
        cp.start()

    def edge_fill(c0, c1, strip):
        edge_value = jnp.where(
            row == 0,
            jnp.broadcast_to(c0[:, :1], (8, LANES)),
            jnp.broadcast_to(c1[:, LANES - 1 :], (8, LANES)),
        )
        return jnp.where(ghost, edge_value, strip)

    def forward(values):
        rolled = [pltpu.roll(v, LANES - 1, 1) for v in values]
        return [jnp.where(last_lane, rolled[(k + 1) % 3], rolled[k]) for k in range(3)]

    def backward(values):
        rolled = [pltpu.roll(v, 1, 1) for v in values]
        return [jnp.where(first_lane, rolled[(k + 2) % 3], rolled[k]) for k in range(3)]

    def stage(lv, cur, old, dst, margin, a, c0, last):
        begin, end = HALO - margin, HALO + CELLS + margin
        along = 2 if last else 3

        def slopes(i):
            o = begin - 1 + 8 * i
            for c in range(NC):
                u = [cur[lv, c, k, pl.ds(o, 8), :] for k in range(3)]
                ahead, behind = forward(u), backward(u)
                for k in range(3):
                    rr[c, k, pl.ds(o, 8), :] = u[k] - 0.5 * minmod(u[k] - behind[k], ahead[k] - u[k])
                for k in range(along):
                    up = cur[lv, c, k, pl.ds(o + 1, 8), :]
                    um = cur[lv, c, k, pl.ds(o - 1, 8), :]
                    hp[c, k, pl.ds(o, 8), :] = 0.5 * minmod(u[k] - um, up - u[k])

        def fluxes(i):
            o = begin - 1 + 8 * i
            right_of = [forward([rr[c, k, pl.ds(o, 8), :] for k in range(3)]) for c in range(NC)]
            for k in range(3):
                here = [cur[lv, c, k, pl.ds(o, 8), :] for c in range(NC)]
                if k < along:
                    left = [here[c] + hp[c, k, pl.ds(o, 8), :] for c in range(NC)]
                    right = [
                        cur[lv, c, k, pl.ds(o + 1, 8), :] - hp[c, k, pl.ds(o + 1, 8), :] for c in range(NC)
                    ]
                    for c, g in enumerate(twice_face(left, right, 0)):
                        gp[c, k, pl.ds(o, 8), :] = g
                left = [here[c] + (here[c] - rr[c, k, pl.ds(o, 8), :]) for c in range(NC)]
                right = [right_of[c][k] for c in range(NC)]
                for c, g in enumerate(twice_face(left, right, 1)):
                    gr[c, k, pl.ds(o, 8), :] = g

        def update(i):
            o = begin + 8 * i
            here = [[cur[lv, c, k, pl.ds(o, 8), :] for k in range(along)] for c in range(NC)]
            turn = [spin[k] for k in range(along)]
            for c in range(NC):
                faces = [gr[c, k, pl.ds(o, 8), :] for k in range(3)]
                below = backward(faces)
                news = []
                for k in range(along):
                    change = (gp[c, k, pl.ds(o, 8), :] - gp[c, k, pl.ds(o - 1, 8), :]) + (
                        faces[k] - below[k]
                    )
                    new = c0 * here[c][k] - (0.5 * DT * c0) * change
                    if a:
                        new = new + a * old[lv, c, k, pl.ds(o, 8), :]
                    if c == 1:
                        new = new - (0.5 * DT * c0) * turn[k] * here[2][k]
                    elif c == 2:
                        new = new + (2.0 * DT * c0) * turn[k] * here[1][k]
                    elif c == 3:
                        new = new - (1.5 * DT * c0) * turn[k] * here[4][k]
                    news.append(new)
                if not last:
                    news[2] = edge_fill(*news)
                for k in range(along):
                    dst(c, k, o, news[k])

        faces = end - begin + 1
        loop(-(-(faces + 1) // 8), slopes)
        loop(-(-faces // 8), fluxes)
        loop(-(-(end - begin) // 8), update)

    def step(lv, land):
        def into(ref, offset):
            def put(c, k, o, value):
                ref[lv, c, k, pl.ds(o + offset, 8), :] = value
            return put

        stage(lv, u0, u0, into(ua, 0), 4, 0.0, 1.0, False)
        stage(lv, ua, u0, into(ub, 0), 2, 0.75, 0.25, False)
        stage(lv, ub, u0, into(land, OWN - HALO), 0, 1.0 / 3.0, 2.0 / 3.0, True)

    def shift_up(tiles, togo, top):
        for b in range(top, -1, -1):
            chosen = (lax.shift_right_logical(togo, b) & 1) == 1
            if b > 2:
                jump = 2 ** (b - 3)
                tiles = [jnp.where(chosen, tiles[t + jump], tiles[t]) for t in range(len(tiles) - jump)]
            else:
                block = jnp.concatenate(tiles, axis=0)
                block = pltpu.roll(block, block.shape[0] - 2**b, 0)
                tiles = [jnp.where(chosen, block[8 * t : 8 * t + 8], tiles[t]) for t in range(len(tiles))]
        return tiles[:-1]

    def both(ref, k):
        return jnp.broadcast_to(ref[:, pl.ds(LANES * k, LANES)], (8, LANES))

    for cp in tables:
        cp.wait()
    for k in range(2):
        spin[k] = both(rot, k)
    spin[2] = jnp.where(lane < 64, both(prot, 0), both(prot, 1))
    for lv in range(LV):
        for cp in first(lv):
            cp.wait()

        def strips(t):
            rows = pl.ds(8 * t, 8)
            packed = got1[lv, rows, :]
            for c in range(NC):
                u0[lv, c, 2, rows, :] = edge_fill(
                    u0[lv, c, 0, rows, :], u0[lv, c, 1, rows, :], unpack(packed, c)
                )

        loop(ROWS // 8, strips)
        step(lv, land1)
        on_moved(land1, plan_mid, lv, send3, recv3, "start")
        pack_edges(land1, pack2, lv, OWN)
        for cp in second(lv):
            cp.start()

    def shifted(land, lv, c, ch, plan, lead, count):
        base = jnp.where(row == 0, plan[0, ch][0], plan[1, ch][0])
        togo = (SMAX - base) - both(sft, ch)
        tiles = [land[lv, c, ch, pl.ds(base + lead + 8 * t, 8), :] for t in range(count + 4)]
        return shift_up(tiles, togo, 4)

    near = jnp.where(row == 0, both(psft, 0), both(psft, 1))
    packed_togo = jnp.zeros((8, LANES), jnp.int32)
    for c in range(NC):
        packed_togo = jnp.where(slot[c], 24 - pltpu.roll(near, 8 * c + 8 * row, 1), packed_togo)
    for lv in range(LV):
        on_moved(land1, plan_mid, lv, send3, recv3, "wait")
        for c in range(NC):
            for ch in range(2):
                for t, tile in enumerate(shifted(land1, lv, c, ch, plan_mid, 0, ROWS // 8)):
                    u0[lv, c, ch, pl.ds(8 * t, 8), :] = tile
        for cp in second(lv):
            cp.wait()
        tiles = [got2[lv, pl.ds(8 * t, 8), :] for t in range(ROWS // 8 + 1)]
        for t, tile in enumerate(shift_up(tiles, packed_togo & 7, 2)):
            rows = pl.ds(8 * t, 8)
            for c in range(NC):
                u0[lv, c, 2, rows, :] = edge_fill(
                    u0[lv, c, 0, rows, :], u0[lv, c, 1, rows, :], unpack(tile, c)
                )
        step(lv, land2)
        on_moved(land2, plan_end, lv, send4, recv4, "start")

    for lv in range(LV):
        on_moved(land2, plan_end, lv, send4, recv4, "wait")
        for c in range(NC):
            for ch in range(2):
                for t, tile in enumerate(shifted(land2, lv, c, ch, plan_end, 8, CELLS // 8)):
                    out[c, lv, pl.ds(8 * t, 8), pl.ds(LANES * ch, LANES)] = tile


def body(density, momentum, magnetic, rotation, shifts):
    block = pltpu.VMEM((LV, NC, 3, TALL, LANES), F32)
    flat = pltpu.VMEM((NC, 3, TALL, LANES), F32)
    land = pltpu.VMEM((LV, NC, 2, LAND, LANES), F32)
    dma = pltpu.SemaphoreType.DMA
    vmem = pl.BlockSpec(memory_space=pltpu.VMEM)
    fields = pl.pallas_call(
        kernel,
        out_shape=jax.ShapeDtypeStruct((NC,) + density.shape, F32),
        in_specs=[vmem] * 5,
        out_specs=vmem,
        scratch_shapes=[
            block, block, block, land, land,
            pltpu.VMEM((LV, CELLS, LANES), F32),
            pltpu.VMEM((LV, CELLS, LANES), F32),
            pltpu.VMEM((LV, ROWS, LANES), F32),
            pltpu.VMEM((LV, 2 * CELLS, LANES), F32),
            pltpu.VMEM((1, 2 * LANES), F32),
            pltpu.VMEM((1, 2 * LANES), jnp.int32),
            flat, flat, flat, flat,
            pltpu.VMEM((3, 8, LANES), F32),
            dma((LV, 5)), dma((LV, 5)), dma((LV, 2)), dma((LV, 2)),
            dma((LV, 2, HOPS)), dma((LV, 2, HOPS)), dma((LV, 2, HOPS)), dma((LV, 2, HOPS)),
            dma((2,)), dma((2,)),
        ],
        compiler_params=pltpu.CompilerParams(collective_id=0, has_side_effects=True),
        name="mhd_steps",
    )(density, momentum, magnetic, rotation[None], shifts[None])
    return fields[0], fields[1:3], fields[3:5]


def solution(mesh):
    placed = (
        P(None, "phi", "row"),
        P(None, None, "phi", "row"),
        P(None, None, "phi", "row"),
        P("row"),
        P("row"),
    )
    return jax.shard_map(
        body,
        mesh=mesh,
        in_specs=placed,
        out_specs=(P(None, "phi", "row"), P(None, None, "phi", "row"), P(None, None, "phi", "row")),
        check_vma=False,
    )
```

```python
import jax
import jax.numpy as jnp
import numpy as np
from jax import lax
from jax.experimental import pallas as pl
from jax.experimental.pallas import tpu as pltpu
from jax.sharding import PartitionSpec as P

SMIN, SMAX = 8, 56
NR = 512
DT = 0.08
LV, NC, CELLS, HALO, LANES = 2, 5, 32, 8, 128
ROWS = CELLS + 2 * HALO
TALL = 64
OWN = 64
LAND = 152
HOPS = 2
GROUP = {6: 3, 5: 5, 4: 4}
MESH = pl.DeviceIdType.MESH
F32 = jnp.float32


def smooth(rows):
    d = NR - 1 - np.clip(rows, 0, NR - 1)
    return SMIN + ((SMAX - SMIN - 1) * d * d) // ((NR - 1) * (NR - 1))


def pieces(ghosts):
    plan = []
    for row in range(2):
        b = smooth(row * 256 + np.arange(2 * LANES))
        low, high = int(b.min()), int(b.max() + 1)
        moves = []
        for k in range(1, HOPS + 1):
            begin = max(0, CELLS * k - high - ghosts)
            end = min(CELLS, CELLS + ghosts - low + CELLS * k)
            if begin < end:
                moves.append((k, begin // 8 * 8, -(-end // 8) * 8))
        plan.append(((SMAX - high) // 8 * 8, tuple(moves)))
    return plan


def one_hot(rows, columns, source):
    r = lax.broadcasted_iota(jnp.int32, (rows, columns), 0)
    m = lax.broadcasted_iota(jnp.int32, (rows, columns), 1)
    return jnp.where(r == source(m), 1.0, 0.0).astype(jnp.bfloat16)


def permuted(x, matrix):
    high = x.astype(jnp.bfloat16)
    rest = x - high.astype(F32)
    middle = rest.astype(jnp.bfloat16)
    low = (rest - middle.astype(F32)).astype(jnp.bfloat16)
    parts = [jnp.dot(v, matrix, preferred_element_type=F32) for v in (high, middle, low)]
    return (parts[0] + parts[1]) + parts[2]


def minmod(a, b):
    return jnp.maximum(jnp.minimum(a, b), 0.0) + jnp.minimum(jnp.maximum(a, b), 0.0)


def physical(state, normal):
    rho, mp, mr, bp, br = state
    inv = 1.0 / rho
    mn, mt, bn, bt = (mp, mr, bp, br) if normal == 0 else (mr, mp, br, bp)
    vn, vt = mn * inv, mt * inv
    bn2, bt2 = bn * bn, bt * bt
    fn = mn * vn + (rho + 0.5 * (bt2 - bn2))
    ft = mt * vn - bn * bt
    fb = bt * vn - bn * vt
    fast = 1.0 + (bn2 + bt2) * inv
    speed = jnp.abs(vn) + fast * lax.rsqrt(fast)
    flux = (mn, fn, ft, None, fb) if normal == 0 else (mn, ft, fn, fb, None)
    return flux, speed


def twice_face(left, right, normal):
    fl, al = physical(left, normal)
    fr, ar = physical(right, normal)
    bound = jnp.maximum(al, ar)
    out = []
    for c in range(NC):
        jump = bound * (right[c] - left[c])
        out.append(-jump if fl[c] is None else (fl[c] + fr[c]) - jump)
    return out


def kernel(den, mom, mag, rot, sft, out,
           u0, ua, ub, land, pack1, pack2, got1, got2, prot, psft, split, join, weave, lines, ordered, back, hp, rr, gp, gr, spin,
           send1, recv1, send2, recv2, send3, recv3, send4, recv4, sendx, recvx):
    phi, row = lax.axis_index("phi"), lax.axis_index("row")
    n = lax.axis_size("phi")
    other = 1 - row

    def at(step, r):
        return {"phi": lax.rem(phi + step + n, n), "row": r}

    barrier = pltpu.get_barrier_semaphore()
    greet = [at(k, row) for k in (1, -1, 2, -2)] + [at(k, other) for k in (0, 1, -1)]
    for dev in greet:
        pl.semaphore_signal(barrier, inc=1, device_id=dev, device_id_type=MESH)

    lane = lax.broadcasted_iota(jnp.int32, (8, LANES), 1)
    first_lane, last_lane = lane == 0, lane == LANES - 1
    ghost = jnp.logical_or(
        jnp.logical_and(row == 0, lane >= LANES - 2), jnp.logical_and(row == 1, lane < 2)
    )
    slot = [jnp.logical_and(lane >= 8 * c, lane < 8 * c + 8) for c in range(NC)]

    def source(lv, c):
        if c == 0:
            return den.at[lv]
        return mom.at[c - 1, lv] if c < 3 else mag.at[c - 3, lv]

    def loop(count, body):
        lax.fori_loop(0, count, lambda i, _: (body(i), 0)[1], 0)

    def pack_edges(lv):
        packs = []
        for t in range(CELLS // 8):
            packed = jnp.zeros((8, LANES), F32)
            rows = pl.ds(OWN + 8 * t, 8)
            for c in range(NC):
                for ch in range(2):
                    moved_to = pltpu.roll(land[0, lv, c, ch, rows, :], 8 * c + 4 * ch + 4 * (1 - row), 1)
                    packed = jnp.where(
                        jnp.logical_and(lane >= 8 * c + 4 * ch, lane < 8 * c + 4 * ch + 4), moved_to, packed
                    )
            packs.append(packed)
        pack2[lv] = permuted(jnp.concatenate(packs, axis=0), weave[...])

    def unpack(packed, c):
        return pltpu.roll(packed, LANES - 8 * c - 8 * row, 1)

    half = LANES.bit_length() - 1
    split[...] = one_hot(2 * LANES, 2 * LANES, lambda m: 2 * (m & (LANES - 1)) + (m >> half))
    join[...] = one_hot(2 * LANES, 2 * LANES, lambda m: (m >> 1) + LANES * (m & 1))
    weave[...] = one_hot(LANES, LANES, lambda m: (m & ~7) + 4 * (m & 1) + ((m & 7) >> 1))

    def load(lv):
        for t in range(CELLS // 8):
            packed = jnp.zeros((8, LANES), F32)
            for c in range(NC):
                tile = source(lv, c)[pl.ds(8 * t, 8), :]
                side = jnp.where(row == 0, tile[:, LANES:], tile[:, :LANES])
                packed = jnp.where(slot[c], pltpu.roll(side, 8 * c + 8 * (1 - row), 1), packed)
            pack1[lv, pl.ds(8 * t, 8), :] = packed
        fields = permuted(jnp.concatenate([source(lv, c)[...] for c in range(NC)], axis=0), split[...])
        for c in range(NC):
            for ch in range(2):
                u0[lv, c, ch, pl.ds(HALO, CELLS), :] = fields[
                    CELLS * c : CELLS * (c + 1), LANES * ch : LANES * (ch + 1)
                ]

    loop(LV, load)
    lines[...] = jnp.zeros((16, 2 * LANES), F32)
    lines[pl.ds(0, 1), :] = rot[...]
    lines[pl.ds(8, 1), :] = sft[...].astype(F32)
    ordered[...] = permuted(lines[...], split[...])

    def remote(src, dst, send, recv, dev):
        return pltpu.make_async_remote_copy(
            src_ref=src, dst_ref=dst, send_sem=send, recv_sem=recv, device_id=dev, device_id_type=MESH
        )

    def first(lv):
        top, bottom = pl.ds(HALO + CELLS - 8, 8), pl.ds(HALO, 8)
        above, below = pl.ds(HALO + CELLS, 8), pl.ds(0, 8)
        main = pl.ds(0, 2)
        parts = (
            (u0.at[lv, :, main, top, :], u0.at[lv, :, main, below, :], at(1, row)),
            (u0.at[lv, :, main, bottom, :], u0.at[lv, :, main, above, :], at(-1, row)),
            (pack1.at[lv], got1.at[lv, pl.ds(HALO, CELLS), :], at(0, other)),
            (pack1.at[lv, pl.ds(CELLS - 8, 8), :], got1.at[lv, below, :], at(1, other)),
            (pack1.at[lv, pl.ds(0, 8), :], got1.at[lv, above, :], at(-1, other)),
        )
        return [remote(a, b, send1.at[lv, i], recv1.at[lv, i], dev) for i, (a, b, dev) in enumerate(parts)]

    def second(lv):
        parts = (
            (pack2.at[lv], got2.at[lv, pl.ds(CELLS, CELLS), :], at(0, other)),
            (pack2.at[lv], got2.at[lv, pl.ds(0, CELLS), :], at(1, other)),
        )
        return [remote(a, b, send2.at[lv, i], recv2.at[lv, i], dev) for i, (a, b, dev) in enumerate(parts)]

    def moved(step, plan, lv, row_id, send, recv):
        copies = []
        for ch in range(2):
            for k, r0, r1 in plan[row_id][1]:
                here, there = pl.ds(OWN + r0, r1 - r0), pl.ds(OWN - CELLS * k + r0, r1 - r0)
                copies.append(remote(
                    land.at[step, lv, :, ch, here, :], land.at[step, lv, :, ch, there, :],
                    send.at[lv, ch, k - 1], recv.at[lv, ch, k - 1], at(k, row),
                ))
        return copies

    plan_mid, plan_end = pieces(6), pieces(0)

    def on_moved(step, lv, what):
        plan, send, recv = ((plan_mid, send3, recv3), (plan_end, send4, recv4))[step]
        for row_id in range(2):
            @pl.when(row == row_id)
            def _():
                for cp in moved(step, plan, lv, row_id, send, recv):
                    getattr(cp, what)()

    pl.semaphore_wait(barrier, len(greet))
    tables = [
        remote(rot, prot, sendx.at[0], recvx.at[0], at(0, other)),
        remote(sft, psft, sendx.at[1], recvx.at[1], at(0, other)),
    ]
    for cp in first(0) + tables + first(1):
        cp.start()

    def edge_fill(even, odd, strip):
        edge_value = pltpu.roll(jnp.where(row == 0, even, odd), jnp.where(row == 0, LANES - 1, 1), 1)
        return jnp.where(ghost, edge_value, strip)

    def forward(values):
        even, odd, strip = values
        even, strip = [pltpu.roll(v, LANES - 1, 1) for v in (even, strip)]
        return [odd, jnp.where(last_lane, strip, even), jnp.where(last_lane, even, strip)]

    def backward(values):
        even, odd, strip = values
        odd, strip = [pltpu.roll(v, 1, 1) for v in (odd, strip)]
        return [jnp.where(first_lane, strip, odd), even, jnp.where(first_lane, odd, strip)]

    def stage(lv, cur, old, dst, margin, a, c0, last):
        begin, end = HALO - margin, HALO + CELLS + margin
        along = 2 if last else 3

        def slopes(i):
            o = begin - 1 + 8 * i
            for c in range(NC):
                u = [cur[lv, c, k, pl.ds(o, 8), :] for k in range(3)]
                ahead, behind = forward(u), backward(u)
                for k in range(3):
                    rr[c, k, pl.ds(o, 8), :] = u[k] - 0.5 * minmod(u[k] - behind[k], ahead[k] - u[k])
                for k in range(along):
                    up = cur[lv, c, k, pl.ds(o + 1, 8), :]
                    um = cur[lv, c, k, pl.ds(o - 1, 8), :]
                    hp[c, k, pl.ds(o, 8), :] = 0.5 * minmod(u[k] - um, up - u[k])

        def fluxes(i):
            o = begin - 1 + 8 * i
            right_of = [forward([rr[c, k, pl.ds(o, 8), :] for k in range(3)]) for c in range(NC)]
            for k in range(3):
                here = [cur[lv, c, k, pl.ds(o, 8), :] for c in range(NC)]
                if k < along:
                    left = [here[c] + hp[c, k, pl.ds(o, 8), :] for c in range(NC)]
                    right = [
                        cur[lv, c, k, pl.ds(o + 1, 8), :] - hp[c, k, pl.ds(o + 1, 8), :] for c in range(NC)
                    ]
                    for c, g in enumerate(twice_face(left, right, 0)):
                        gp[c, k, pl.ds(o, 8), :] = g
                left = [here[c] + (here[c] - rr[c, k, pl.ds(o, 8), :]) for c in range(NC)]
                right = [right_of[c][k] for c in range(NC)]
                for c, g in enumerate(twice_face(left, right, 1)):
                    gr[c, k, pl.ds(o, 8), :] = g

        def update(i):
            o = begin + 8 * i
            here = [[cur[lv, c, k, pl.ds(o, 8), :] for k in range(along)] for c in range(NC)]
            turn = [spin[k] for k in range(along)]
            for c in range(NC):
                faces = [gr[c, k, pl.ds(o, 8), :] for k in range(3)]
                below = backward(faces)
                news = []
                for k in range(along):
                    change = (gp[c, k, pl.ds(o, 8), :] - gp[c, k, pl.ds(o - 1, 8), :]) + (
                        faces[k] - below[k]
                    )
                    new = c0 * here[c][k] - (0.5 * DT * c0) * change
                    if a:
                        new = new + a * old[lv, c, k, pl.ds(o, 8), :]
                    if c == 1:
                        new = new - (0.5 * DT * c0) * turn[k] * here[2][k]
                    elif c == 2:
                        new = new + (2.0 * DT * c0) * turn[k] * here[1][k]
                    elif c == 3:
                        new = new - (1.5 * DT * c0) * turn[k] * here[4][k]
                    news.append(new)
                if not last:
                    news[2] = edge_fill(*news)
                for k in range(along):
                    dst(c, k, o, news[k])

        faces = end - begin + 1
        for body, rows in ((slopes, faces + 1), (fluxes, faces), (update, end - begin)):
            count = -(-rows // 8)
            group = GROUP[count]

            def turn(i):
                for j in range(group):
                    body(group * i + j)

            if group == count:
                turn(0)
            else:
                loop(count // group, turn)

    def sections(step, lv):
        def into(ref, offset, lead):
            def put(c, k, o, value):
                ref[(*lead, c, k, pl.ds(o + offset, 8), slice(None))] = value
            return put

        stage(lv, u0, u0, into(ua, 0, (lv,)), 4, 0.0, 1.0, False)
        stage(lv, ua, u0, into(ub, 0, (lv,)), 2, 0.75, 0.25, False)
        stage(lv, ub, u0, into(land, OWN - HALO, (step, lv)), 0, 1.0 / 3.0, 2.0 / 3.0, True)

    def shift_up(tiles, togo, top):
        for b in range(top, -1, -1):
            chosen = (lax.shift_right_logical(togo, b) & 1) == 1
            if b > 2:
                jump = 2 ** (b - 3)
                tiles = [jnp.where(chosen, tiles[t + jump], tiles[t]) for t in range(len(tiles) - jump)]
            else:
                block = jnp.concatenate(tiles, axis=0)
                block = pltpu.roll(block, block.shape[0] - 2**b, 0)
                tiles = [jnp.where(chosen, block[8 * t : 8 * t + 8], tiles[t]) for t in range(len(tiles))]
        return tiles[:-1]

    def both(ref, k):
        return jnp.broadcast_to(ref[:, pl.ds(LANES * k, LANES)], (8, LANES))

    for cp in tables:
        cp.wait()
    for k in range(2):
        spin[k] = jnp.broadcast_to(ordered[pl.ds(0, 1), pl.ds(LANES * k, LANES)], (8, LANES))
    spin[2] = jnp.where(lane < 64, both(prot, 0), both(prot, 1))

    def shifted(step, lv, c, ch, plan, lead, count):
        base = jnp.where(row == 0, plan[0][0], plan[1][0])
        shift = jnp.broadcast_to(ordered[pl.ds(8, 1), pl.ds(LANES * ch, LANES)], (8, LANES))
        togo = (SMAX - base) - shift.astype(jnp.int32)
        tiles = [land[step, lv, c, ch, pl.ds(base + lead + 8 * t, 8), :] for t in range(count + 8)]
        return shift_up(tiles, togo, 5)

    near = jnp.where(row == 0, both(psft, 0), both(psft, 1))
    packed_togo = jnp.zeros((8, LANES), jnp.int32)
    for c in range(NC):
        packed_togo = jnp.where(slot[c], 24 - pltpu.roll(near, 8 * c + 8 * row, 1), packed_togo)

    def turn(i):
        step, lv = lax.div(i, LV), lax.rem(i, LV)

        @pl.when(step == 0)
        def _():
            for cp in first(lv):
                cp.wait()

        @pl.when(step == 1)
        def _():
            on_moved(0, lv, "wait")

            def move(c):
                for ch in range(2):
                    for t, tile in enumerate(shifted(0, lv, c, ch, plan_mid, 0, ROWS // 8)):
                        u0[lv, c, ch, pl.ds(8 * t, 8), :] = tile

            loop(NC, move)
            for cp in second(lv):
                cp.wait()
            tiles = [got2[lv, pl.ds(8 * t, 8), :] for t in range(ROWS // 8 + 1)]
            for t, tile in enumerate(shift_up(tiles, packed_togo & 7, 2)):
                got1[lv, pl.ds(8 * t, 8), :] = tile

        def strips(t):
            rows = pl.ds(8 * t, 8)
            packed = got1[lv, rows, :]
            for c in range(NC):
                u0[lv, c, 2, rows, :] = edge_fill(
                    u0[lv, c, 0, rows, :], u0[lv, c, 1, rows, :], unpack(packed, c)
                )

        loop(ROWS // 8, strips)
        sections(step, lv)

        @pl.when(step == 0)
        def _():
            on_moved(0, lv, "start")
            pack_edges(lv)
            for cp in second(lv):
                cp.start()

        @pl.when(step == 1)
        def _():
            on_moved(1, lv, "start")

    loop(2 * LV, turn)

    def finish(lv):
        on_moved(1, lv, "wait")

        def move(c):
            for ch in range(2):
                for t, tile in enumerate(shifted(1, lv, c, ch, plan_end, 8, CELLS // 8)):
                    back[pl.ds(CELLS * c + 8 * t, 8), pl.ds(LANES * ch, LANES)] = tile

        loop(NC, move)
        fields = permuted(back[...], join[...])
        for c in range(NC):
            out[c, lv] = fields[CELLS * c : CELLS * (c + 1)]

    loop(LV, finish)


def body(density, momentum, magnetic, rotation, shifts):
    block = pltpu.VMEM((LV, NC, 3, TALL, LANES), F32)
    flat = pltpu.VMEM((NC, 3, TALL, LANES), F32)
    land = pltpu.VMEM((2, LV, NC, 2, LAND, LANES), F32)
    dma = pltpu.SemaphoreType.DMA
    vmem = pl.BlockSpec(memory_space=pltpu.VMEM)
    fields = pl.pallas_call(
        kernel,
        out_shape=jax.ShapeDtypeStruct((NC,) + density.shape, F32),
        in_specs=[vmem] * 5,
        out_specs=vmem,
        scratch_shapes=[
            block, block, block, land,
            pltpu.VMEM((LV, CELLS, LANES), F32),
            pltpu.VMEM((LV, CELLS, LANES), F32),
            pltpu.VMEM((LV, ROWS, LANES), F32),
            pltpu.VMEM((LV, 2 * CELLS, LANES), F32),
            pltpu.VMEM((1, 2 * LANES), F32),
            pltpu.VMEM((1, 2 * LANES), jnp.int32),
            pltpu.VMEM((2 * LANES, 2 * LANES), jnp.bfloat16),
            pltpu.VMEM((2 * LANES, 2 * LANES), jnp.bfloat16),
            pltpu.VMEM((LANES, LANES), jnp.bfloat16),
            pltpu.VMEM((16, 2 * LANES), F32),
            pltpu.VMEM((16, 2 * LANES), F32),
            pltpu.VMEM((NC * CELLS, 2 * LANES), F32),
            flat, flat, flat, flat,
            pltpu.VMEM((3, 8, LANES), F32),
            dma((LV, 5)), dma((LV, 5)), dma((LV, 2)), dma((LV, 2)),
            dma((LV, 2, HOPS)), dma((LV, 2, HOPS)), dma((LV, 2, HOPS)), dma((LV, 2, HOPS)),
            dma((2,)), dma((2,)),
        ],
        compiler_params=pltpu.CompilerParams(collective_id=0, has_side_effects=True),
        name="mhd_steps",
    )(density, momentum, magnetic, rotation[None], shifts[None])
    return fields[0], fields[1:3], fields[3:5]


def solution(mesh):
    placed = (
        P(None, "phi", "row"),
        P(None, None, "phi", "row"),
        P(None, None, "phi", "row"),
        P("row"),
        P("row"),
    )
    return jax.shard_map(
        body,
        mesh=mesh,
        in_specs=placed,
        out_specs=(P(None, "phi", "row"), P(None, None, "phi", "row"), P(None, None, "phi", "row")),
        check_vma=False,
    )
```
